256 devices in a mesh: tile: 32 (over z_hi, x, core), head: 8 (over z_lo, y).
Axes of the slice: x: 4, y: 4, z: 8 (z_hi: 4, z_lo: 2; z = z_hi * 2 + z_lo), core: 2. Of those that a mesh axis runs over, the one named last changes fastest.
Arguments:
- queries: bfloat16 [32768, 3072], P(('tile', 'head')), may hold values from -16 to 16
- keys_in: bfloat16 [32768, 3072], P(('tile', 'head')), may hold values from -16 to 16
- values_in: bfloat16 [32768, 3072], P(('tile', 'head')), may hold values from -6 to 6
- grad_out: bfloat16 [32768, 3072], P(('tile', 'head')), may hold values from -6 to 6
- positions: int32 [2, 32768], P(None, ('tile', 'head')), may hold values from 0 to 255
Outputs:
- attended: bfloat16 [32768, 3072], P(('tile', 'head'))
- query_grad: bfloat16 [32768, 3072], P(('tile', 'head'))
- key_grad: bfloat16 [32768, 3072], P(('tile', 'head'))
- value_grad: bfloat16 [32768, 3072], P(('tile', 'head'))
The draws below stay inside these ranges and needn't reach their ends.
All inputs are finite; a program needn't handle non-finite values.
Results may differ from the reference program's by a relative error of at most 0.011.
Values may be sent and summed in bfloat16 or wider, within the bound.
No kernel may reach another device: no remote copies, remote signals or barrier semaphores. Data moves between devices by JAX's collectives and lax.ppermute only.
A program may use at most 128 MiB of HBM per device.

```python
import math
import jax
import jax.numpy as jnp
from jax import lax

HEAD_DIM = 128
WIDTH = 3072
TILE_TOK = 256
GRID_COLS = 8
TILES = 128
GRID_ROWS = 16
TOKENS = 32768
POS_SPAN = 256


def draw_pair(key):
    shape_all = (TOKENS, WIDTH)
    query_part = jnp.clip(jax.random.normal(jax.random.fold_in(key, 31), shape_all), -6.0, 6.0)
    key_part = jnp.clip(jax.random.normal(jax.random.fold_in(key, 32), shape_all), -6.0, 6.0)
    return (query_part, key_part)


def draw_queries(key, part):
    return draw_pair(key)[0].astype(jnp.bfloat16)


def draw_keys_in(key, part):
    return draw_pair(key)[1].astype(jnp.bfloat16)


def set_ends(array, key, low, top_value):
    place = [jax.random.randint(jax.random.fold_in(key, axis), (), 0, length) for axis, length in enumerate(array.shape)]
    main_axis = array.shape.index(max(array.shape))
    neighbour = place[:main_axis] + [(place[main_axis] + 1) % array.shape[main_axis]] + place[main_axis + 1:]
    return array.at[tuple(place)].set(low).at[tuple(neighbour)].set(top_value)


def steps_of(rng, dims, cuts, smallest, top_value):
    loudness, own = 1.0, jax.random.fold_in(rng, 6)
    for axis_at, parts in cuts:
        draws = jnp.exp(jax.random.uniform(jax.random.fold_in(own, axis_at), (parts,), jnp.float32, smallest / len(cuts), top_value / len(cuts)))
        loudness = loudness * jnp.repeat(draws, dims[axis_at] // parts).reshape([-1 if axis == axis_at else 1 for axis in range(len(dims))])
    return loudness


def normal_values(stream_key, dims, deviation, bound, pieces=(), held_as=jnp.bfloat16):
    gain = steps_of(stream_key, dims, pieces, -0.22, 0.18) if pieces else 1.0
    entries = jax.random.normal(stream_key, dims, jnp.float32) * deviation * gain
    return jnp.minimum(jnp.maximum(entries, -bound), bound).astype(held_as)


def setup_inputs(seed: int = 0) -> dict:
    seeds = jax.random.split(jax.random.key(seed), 6)
    queries = draw_queries(jax.random.fold_in(seeds[5], 71), 0)
    keys_in = draw_keys_in(jax.random.fold_in(seeds[5], 71), 0)
    values_in = normal_values(seeds[2], (TOKENS, WIDTH), 1.0, 6.0, ((0, 256),))
    grad_out = normal_values(seeds[3], (TOKENS, WIDTH), 1.0, 6.0, ((0, 256),))
    positions = set_ends(jax.random.randint(seeds[4], (2, TOKENS), 0, POS_SPAN), jax.random.fold_in(seeds[4], 1), 0, POS_SPAN - 1).astype(jnp.int32)
    return dict(queries=queries, keys_in=keys_in, values_in=values_in, grad_out=grad_out, positions=positions)


THETA = 10000.0


def angle_tables(row_ids, col_ids):
    turned = 7 * HEAD_DIM // 16
    unturned = HEAD_DIM - 2 * turned
    slot_ids = lax.iota(jnp.int32, HEAD_DIM)
    offset = slot_ids - unturned
    by_column = offset >= turned
    within = jnp.where(by_column, offset - turned, offset)
    paired = jnp.maximum(within, 0) // 2
    frequency = jnp.exp(paired.astype(jnp.float32) * (-2.0 * math.log(THETA) / turned))
    chosen = jnp.where(by_column[None, :], col_ids[:, None], row_ids[:, None]).astype(jnp.float32)
    angles = chosen * frequency[None, :]
    active = (offset >= 0)[None, :]
    cosine = jnp.where(active, jnp.cos(angles), 1.0)
    parity = jnp.where(within % 2 == 0, -1.0, 1.0)
    signed_sine = jnp.where(active, jnp.sin(angles) * parity[None, :], 0.0)
    return cosine, signed_sine


def swap_matrix():
    slot_ids = lax.iota(jnp.int32, HEAD_DIM)
    partner = jnp.bitwise_xor(slot_ids, 1)
    return (slot_ids[:, None] == partner[None, :]).astype(jnp.float32)


def turn_forward(tensor, cosine, signed_sine, matrix):
    flattened = tensor.reshape(-1, HEAD_DIM)
    swapped = jnp.dot(flattened, matrix, precision=lax.Precision.HIGHEST).reshape(tensor.shape)
    return tensor * cosine[:, None, :] + swapped * signed_sine[:, None, :]


def turn_back(gradient, cosine, signed_sine, matrix):
    flattened = (gradient * signed_sine[:, None, :]).reshape(-1, HEAD_DIM)
    swapped = jnp.dot(flattened, matrix, precision=lax.Precision.HIGHEST).reshape(gradient.shape)
    return gradient * cosine[:, None, :] + swapped


def query_kernel(q_tile, g_tile, near_keys, near_values, usable):
    highest = lax.Precision.HIGHEST
    inv_root = HEAD_DIM ** -0.5
    scores = jnp.einsum("qhd,khd->hqk", q_tile.astype(jnp.float32), near_keys.astype(jnp.float32), precision=highest) * inv_root
    scores = jnp.where(usable[None, None, :], scores, -jnp.inf)
    row_max = jnp.max(scores, axis=-1, keepdims=True)
    log_norm = row_max + jnp.log(jnp.sum(jnp.exp(scores - row_max), axis=-1, keepdims=True))
    weights = jnp.exp(scores - log_norm)
    weights_half = lax.optimization_barrier(weights.astype(jnp.bfloat16))
    attended = jnp.einsum("hqk,khd->qhd", weights_half.astype(jnp.float32), near_values.astype(jnp.float32), precision=highest)
    attended = lax.optimization_barrier(attended.astype(jnp.bfloat16))
    row_dots = jnp.sum(g_tile.astype(jnp.float32) * attended.astype(jnp.float32), axis=-1).T
    weight_grad = jnp.einsum("qhd,khd->hqk", g_tile.astype(jnp.float32), near_values.astype(jnp.float32), precision=highest)
    dscore = lax.optimization_barrier((weights * (weight_grad - row_dots[:, :, None]) * inv_root).astype(jnp.bfloat16))
    dq_rot = jnp.einsum("hqk,khd->qhd", dscore.astype(jnp.float32), near_keys.astype(jnp.float32), precision=highest)
    return attended, log_norm[:, :, 0], row_dots, dq_rot


def key_kernel(k_tile, v_tile, near_queries, near_grads, near_norms, near_dots, usable):
    highest = lax.Precision.HIGHEST
    inv_root = HEAD_DIM ** -0.5
    scores = jnp.einsum("khd,qhd->hkq", k_tile.astype(jnp.float32), near_queries.astype(jnp.float32), precision=highest) * inv_root
    weights = jnp.where(usable[None, None, :], jnp.exp(scores - near_norms[:, None, :]), 0.0)
    weights_half = lax.optimization_barrier(weights.astype(jnp.bfloat16))
    dv_part = jnp.einsum("hkq,qhd->khd", weights_half.astype(jnp.float32), near_grads.astype(jnp.float32), precision=highest)
    weight_grad = jnp.einsum("khd,qhd->hkq", v_tile.astype(jnp.float32), near_grads.astype(jnp.float32), precision=highest)
    dscore = lax.optimization_barrier((weights * (weight_grad - near_dots[:, None, :]) * inv_root).astype(jnp.bfloat16))
    dk_part = jnp.einsum("hkq,qhd->khd", dscore.astype(jnp.float32), near_queries.astype(jnp.float32), precision=highest)
    return dk_part, dv_part


def reference(queries, keys_in, values_in, grad_out, positions):
    head_count = queries.shape[1] // HEAD_DIM
    shape_all = (TOKENS, head_count, HEAD_DIM)
    cosine, signed_sine = angle_tables(positions[0], positions[1])
    matrix = swap_matrix()
    q_rot = turn_forward(queries.astype(jnp.float32).reshape(shape_all), cosine, signed_sine, matrix)
    q_rot = lax.optimization_barrier(q_rot.astype(jnp.bfloat16))
    k_rot = turn_forward(keys_in.astype(jnp.float32).reshape(shape_all), cosine, signed_sine, matrix)
    k_rot = lax.optimization_barrier(k_rot.astype(jnp.bfloat16))
    tile_shape = (TILES, TILE_TOK, head_count, HEAD_DIM)
    q_tiles = q_rot.reshape(tile_shape)
    k_tiles = k_rot.reshape(tile_shape)
    v_tiles = values_in.reshape(tile_shape)
    g_tiles = grad_out.reshape(tile_shape)

    def near_of(tile_at):
        row_of = tile_at // GRID_COLS
        col_of = tile_at % GRID_COLS
        starts = []
        flag_list = []
        for row_step in (-1, 0, 1):
            for col_step in (-1, 0, 1):
                starts.append(jnp.clip(tile_at + row_step * GRID_COLS + col_step, 0, TILES - 1).astype(jnp.int32))
                near_flag = (row_of + row_step >= 0) & (row_of + row_step < GRID_ROWS) & (col_of + col_step >= 0) & (col_of + col_step < GRID_COLS)
                flag_list.append(jnp.broadcast_to(near_flag, (TILE_TOK,)))
        return starts, jnp.concatenate(flag_list)

    def gather_near(tile_stack, starts, axis_dim):
        return jnp.concatenate([lax.dynamic_index_in_dim(tile_stack, start_at, 0, keepdims=False) for start_at in starts], axis=axis_dim)

    def query_pass(tile_at):
        starts, usable = near_of(tile_at)
        q_tile = lax.dynamic_index_in_dim(q_tiles, tile_at, 0, keepdims=False)
        g_tile = lax.dynamic_index_in_dim(g_tiles, tile_at, 0, keepdims=False)
        return query_kernel(q_tile, g_tile, gather_near(k_tiles, starts, 0), gather_near(v_tiles, starts, 0), usable)

    attended, log_norm, row_dots, dq_rot = lax.map(query_pass, jnp.arange(TILES, dtype=jnp.int32))

    def key_pass(tile_at):
        starts, usable = near_of(tile_at)
        k_tile = lax.dynamic_index_in_dim(k_tiles, tile_at, 0, keepdims=False)
        v_tile = lax.dynamic_index_in_dim(v_tiles, tile_at, 0, keepdims=False)
        return key_kernel(k_tile, v_tile, gather_near(q_tiles, starts, 0), gather_near(g_tiles, starts, 0), gather_near(log_norm, starts, 1), gather_near(row_dots, starts, 1), usable)

    dk_rot, dv_sum = lax.map(key_pass, jnp.arange(TILES, dtype=jnp.int32))
    query_grad = turn_back(dq_rot.reshape(shape_all), cosine, signed_sine, matrix).astype(jnp.bfloat16).reshape(TOKENS, -1)
    key_grad = turn_back(dk_rot.reshape(shape_all), cosine, signed_sine, matrix).astype(jnp.bfloat16).reshape(TOKENS, -1)
    value_grad = dv_sum.reshape(TOKENS, -1).astype(jnp.bfloat16)
    return attended.reshape(TOKENS, -1), query_grad, key_grad, value_grad
```

```python
import functools
import math

import jax
import jax.numpy as jnp
from jax import lax
from jax.experimental import pallas as pl
from jax.experimental.pallas import tpu as pltpu
from jax.sharding import PartitionSpec as P


HEAD_DIM = 128
TILE_TOK = 256
THETA = 10000.0
INV_ROOT = HEAD_DIM ** (-0.5)
PAIR = 2 * HEAD_DIM
BF16 = jnp.bfloat16
F32 = jnp.float32


def angle_tables(row_ids, col_ids):
    turned = 7 * HEAD_DIM // 16
    unturned = HEAD_DIM - 2 * turned
    slot_ids = lax.iota(jnp.int32, HEAD_DIM)
    offset = slot_ids - unturned
    by_column = offset >= turned
    within = jnp.where(by_column, offset - turned, offset)
    paired = jnp.maximum(within, 0) // 2
    frequency = jnp.exp(paired.astype(F32) * (-2.0 * math.log(THETA) / turned))
    chosen = jnp.where(by_column[None, :], col_ids[:, None], row_ids[:, None]).astype(F32)
    angles = chosen * frequency[None, :]
    active = (offset >= 0)[None, :]
    cosine = jnp.where(active, jnp.cos(angles), 1.0)
    parity = jnp.where(within % 2 == 0, -1.0, 1.0)
    signed_sine = jnp.where(active, jnp.sin(angles) * parity[None, :], 0.0)
    return (cosine, signed_sine)


def swap_matrix():
    slots = lax.broadcasted_iota(jnp.int32, (HEAD_DIM, HEAD_DIM), 0)
    partner = jnp.bitwise_xor(lax.broadcasted_iota(jnp.int32, (HEAD_DIM, HEAD_DIM), 1), 1)
    return (slots == partner).astype(F32).astype(BF16)


def dot(a, b, dims):
    return lax.dot_general(a, b, (dims, ((), ())), preferred_element_type=F32)


def turn(x, cosine, sine):
    swapped = dot(x, swap_matrix(), ((1,), (0,)))
    return x.astype(F32) * cosine + swapped * sine


def pack_body(members, turned_ref, plain_ref, cos_ref, sin_ref, out_ref):
    cosine = cos_ref[...]
    sine = sin_ref[...]
    heads = turned_ref.shape[1] // HEAD_DIM // out_ref.shape[0]
    for group in range(out_ref.shape[0]):
        for n, head in enumerate(members):
            at = (group * heads + head) * HEAD_DIM
            cols = slice(at, at + HEAD_DIM)
            low = slice(n * PAIR, n * PAIR + HEAD_DIM)
            high = slice(n * PAIR + HEAD_DIM, (n + 1) * PAIR)
            out_ref[group, :, low] = turn(turned_ref[:, cols], cosine, sine).astype(BF16)
            out_ref[group, :, high] = plain_ref[:, cols]


def pack(turned, plain, cosine, sine, groups, members):
    rows, wide = turned.shape
    block = wide // PACK_STEPS
    width = len(members) * PAIR
    token_block = pl.BlockSpec((rows, block), lambda h: (0, h))
    table_block = pl.BlockSpec((rows, HEAD_DIM), lambda h: (0, 0))
    return pl.pallas_call(
        functools.partial(pack_body, members),
        grid=(PACK_STEPS,),
        in_specs=[token_block] * 2 + [table_block] * 2,
        out_specs=pl.BlockSpec((groups // PACK_STEPS, rows, width), lambda h: (h, 0, 0)),
        out_shape=jax.ShapeDtypeStruct((groups, rows, width), BF16),
        name="pack",
    )(turned, plain, cosine, sine)


def unpack_body(chunks, turn_first, *refs):
    size = len(chunks)
    cos_ref, back_ref, low_out, high_out = refs[size:]
    cosine = cos_ref[...]
    back_sine = back_ref[...]
    heads = sum(len(members) for members in chunks)
    for group in range(refs[0].shape[0]):
        for c, members in enumerate(chunks):
            for n, head in enumerate(members):
                at = (group * heads + head) * HEAD_DIM
                cols = slice(at, at + HEAD_DIM)
                low = refs[c][group, :, n * PAIR : n * PAIR + HEAD_DIM]
                high = refs[c][group, :, n * PAIR + HEAD_DIM : (n + 1) * PAIR]
                if turn_first:
                    low = turn(low, cosine, back_sine).astype(BF16)
                else:
                    high = turn(high, cosine, back_sine).astype(BF16)
                low_out[:, cols] = low
                high_out[:, cols] = high


def unpack(parts, cosine, back_sine, groups, chunks, turn_first):
    rows = parts[0].shape[1]
    wide = groups * sum(len(members) for members in chunks) * HEAD_DIM
    token_block = pl.BlockSpec((rows, wide // PACK_STEPS), lambda h: (0, h))
    table_block = pl.BlockSpec((rows, HEAD_DIM), lambda h: (0, 0))
    return pl.pallas_call(
        functools.partial(unpack_body, chunks, turn_first),
        grid=(PACK_STEPS,),
        in_specs=[
            pl.BlockSpec((groups // PACK_STEPS, rows, part.shape[2]), lambda h: (h, 0, 0))
            for part in parts
        ]
        + [table_block] * 2,
        out_specs=[token_block] * 2,
        out_shape=[jax.ShapeDtypeStruct((rows, wide), BF16)] * 2,
        name="unpack",
    )(*parts, cosine, back_sine)


def attend_body(number, head, heads, relays, place, qg_ref, own_ref, up_ref, down_ref, edge_ref, *refs):
    relay_refs, refs = refs[:relays], refs[relays:]
    out_ref, own_out, up_out, down_out, edge_out = refs[:5]
    copies, (sums, edge_sums, score, prob, turned) = refs[5 : 5 + 2 * relays], refs[5 + 2 * relays :]
    side = place[0]
    valid = (place[1] == 1, None, place[2] == 1)
    factor = INV_ROOT * math.log2(math.e)
    key_refs = (up_ref, own_ref, down_ref)
    if relays:
        for flag, near_ref, copy in zip((place[3], place[4]), (up_ref, down_ref), copies):

            @pl.when(flag == 1)
            def _():
                copy[...] = relay_refs[0][...]

            @pl.when(flag == 0)
            def _():
                copy[...] = near_ref[...]

        key_refs = (copies[0], own_ref, copies[1])
    key_outs = (up_out, own_out, down_out)

    def tokens(tile, count=1):
        return pl.ds(pl.multiple_of(tile * TILE_TOK, TILE_TOK), count * TILE_TOK)

    def head_step(n):
        def lanes(index, half):
            return pl.ds(pl.multiple_of(index * PAIR + half * HEAD_DIM, HEAD_DIM), HEAD_DIM)

        def plan(j):
            if j == 0:
                return [(False, tokens(side * (number - 2), 2), 0, 2)]
            if j == number - 1:
                return [(False, tokens((1 - side) * (number - 2), 2), 0, 2), (True, None, 2, 1)]
            return [(False, tokens(j - 1 + side * (number - 1 - 2 * j), 3), 0, 3)]

        def keys(row, span, half):
            if span[0]:
                return edge_ref[row * TILE_TOK : (row + 1) * TILE_TOK, lanes(n, half)]
            return key_refs[row][span[1], lanes(n, half)]

        def held(span):
            return slice(span[2] * TILE_TOK, (span[2] + span[3]) * TILE_TOK)

        def forward(j):
            slot = j % 2
            mine = tokens(j + side * (number - 1 - 2 * j))
            q_t = qg_ref[mine, lanes(head + n, 0)].astype(F32).T.astype(BF16)
            tops, totals, parts = [], [], []
            for row in range(3):
                top = None
                for span in plan(j):
                    s = dot(keys(row, span, 0), q_t, ((1,), (0,)))
                    score[slot, row, held(span), :] = s
                    peak = jnp.max(s, axis=0, keepdims=True)
                    top = peak if top is None else jnp.maximum(top, peak)
                total, part = 0.0, 0.0
                for span in plan(j):
                    e = jnp.exp2((score[slot, row, held(span), :] - top) * factor)
                    e_half = e.astype(BF16)
                    prob[slot, row, held(span), :] = e_half
                    total = total + jnp.sum(e, axis=0, keepdims=True)
                    part = part + dot(keys(row, span, 1), e_half, ((0,), (0,)))
                tops.append(top)
                totals.append(total)
                parts.append(part)
            best = tops[1]
            for row in (0, 2):
                best = jnp.where(valid[row], jnp.maximum(best, tops[row]), best)
            scales = []
            for row in range(3):
                scale = jnp.exp2(jnp.minimum(tops[row] - best, 0.0) * factor)
                if valid[row] is not None:
                    scale = jnp.where(valid[row], scale, 0.0)
                scales.append(scale)
            inverse = 1.0 / sum(t * c for t, c in zip(totals, scales))
            scales = [c * inverse for c in scales]
            att_t = sum(p * c for p, c in zip(parts, scales))
            out_ref[mine, lanes(n, 0)] = att_t.T.astype(BF16)
            turned[slot] = att_t.astype(BF16).astype(F32)
            return scales

        def backward(j, scales):
            slot = j % 2
            mine = tokens(j + side * (number - 1 - 2 * j))
            q_tile = qg_ref[mine, lanes(head + n, 0)]
            g_t = qg_ref[mine, lanes(head + n, 1)].astype(F32).T
            att_t = turned[slot]
            dq_t = 0.0
            for row in range(3):
                scaled_t = (g_t * scales[row]).astype(BF16)
                wide_t = scaled_t.astype(F32)
                scaled = wide_t.T.astype(BF16)
                row_dots = jnp.sum(wide_t * att_t, axis=0, keepdims=True)
                for span in plan(j):
                    weights = prob[slot, row, held(span), :]
                    dp = dot(keys(row, span, 1), scaled_t, ((1,), (0,)))
                    ds = weights * (dp - row_dots).astype(BF16)
                    dk = dot(ds, q_tile, ((1,), (0,)))
                    dv = dot(weights, scaled, ((1,), (0,)))
                    dq_t = dq_t + dot(keys(row, span, 0), ds, ((0,), (0,)))
                    if span[0]:
                        edge_sums[row, :, :HEAD_DIM] = dk
                        edge_sums[row, :, HEAD_DIM:] = dv
                    else:
                        sums[row, span[1], :HEAD_DIM] += dk
                        sums[row, span[1], HEAD_DIM:] += dv
            out_ref[mine, lanes(n, 1)] = (dq_t * INV_ROOT).T.astype(BF16)

        sums[...] = jnp.zeros(sums.shape, F32)
        scales = forward(0)
        for j in range(number):
            ahead = forward(j + 1) if j + 1 < number else None
            backward(j, scales)
            scales = ahead
        for row in range(3):
            key_outs[row][:, lanes(n, 0)] = (sums[row, :, :HEAD_DIM] * INV_ROOT).astype(BF16)
            key_outs[row][:, lanes(n, 1)] = sums[row, :, HEAD_DIM:].astype(BF16)
            rows = slice(row * TILE_TOK, (row + 1) * TILE_TOK)
            edge_out[rows, lanes(n, 0)] = (edge_sums[row, :, :HEAD_DIM] * INV_ROOT).astype(BF16)
            edge_out[rows, lanes(n, 1)] = edge_sums[row, :, HEAD_DIM:].astype(BF16)

    if heads == 1:
        head_step(0)
    else:
        pl.loop(0, heads)(head_step)


def attend(place, head, qg, own, up, down, edge, *relay):
    rows, width = own.shape
    number = rows // TILE_TOK
    vmem = pl.BlockSpec(memory_space=pltpu.VMEM)
    tiles = jax.ShapeDtypeStruct((rows, width), BF16)
    edges = jax.ShapeDtypeStruct((3 * TILE_TOK, width), BF16)
    return pl.pallas_call(
        functools.partial(attend_body, number, head, width // PAIR, len(relay)),
        in_specs=[pl.BlockSpec(memory_space=pltpu.SMEM)] + [vmem] * (5 + len(relay)),
        out_specs=[vmem] * 5,
        scratch_shapes=[
            *[pltpu.VMEM((rows, width), BF16)] * (2 * len(relay)),
            pltpu.VMEM((3, rows, PAIR), F32),
            pltpu.VMEM((3, TILE_TOK, PAIR), F32),
            pltpu.VMEM((2, 3, 3 * TILE_TOK, TILE_TOK), F32),
            pltpu.VMEM((2, 3, 3 * TILE_TOK, TILE_TOK), BF16),
            pltpu.VMEM((2, HEAD_DIM, TILE_TOK), F32),
        ],
        out_shape=[tiles, tiles, tiles, tiles, edges],
        compiler_params=pltpu.CompilerParams(vmem_limit_bytes=40 << 20),
        name="attend",
    )(place, qg, own, up, down, edge, *relay)


CHUNKS = ((0, 1), (2,))
PACK_STEPS = 2
RELAYED = (0,)
RUN = 8


def local(queries, keys_in, values_in, grad_out, positions):
    groups = lax.axis_size("head")
    count = lax.axis_size("tile")
    tile_at = lax.axis_index("tile")
    head_at = lax.axis_index("head")
    number = groups * queries.shape[0] // TILE_TOK
    chunks = CHUNKS
    side = tile_at % 2
    far = head_at >= groups // 2
    at_right = tile_at % RUN >= RUN - 2
    has_up = tile_at >= 2
    has_down = tile_at < count - 2
    relay_up = far & (tile_at % RUN < 2) & has_up
    relay_down = far & at_right & has_down
    place = jnp.stack([x.astype(jnp.int32) for x in (side, has_up, has_down, relay_up, relay_down)])
    edge_start = (number - 1) * (1 - side) * TILE_TOK
    cosine, sine = angle_tables(positions[0], positions[1])
    back_sine = jnp.where(lax.iota(jnp.int32, HEAD_DIM) % 2 == 0, jnp.roll(sine, -1, 1), jnp.roll(sine, 1, 1))

    def pairs(moves):
        return [(t * groups + h, u * groups + h) for t, u, h in moves]

    steps = [(t, t + 2, h) for t in range(count - 2) for h in range(groups)]
    relayed = [m for m in steps if m[0] // RUN != m[1] // RUN and m[2] >= groups // 2]
    direct = [m for m in steps if m not in relayed]
    turn_at = RUN - 2
    first_pairs = pairs(
        [(t, t - turn_at, h) for t, u, h in relayed] + [(u, u + turn_at, h) for t, u, h in relayed]
    )
    second_pairs = pairs(
        [(t - turn_at, u, h) for t, u, h in relayed] + [(u + turn_at, t, h) for t, u, h in relayed]
    )
    swap_pairs = pairs([(t, t ^ 1, h) for t in range(count) for h in range(groups)])

    def across(value):
        return lax.all_to_all(value, "head", split_axis=0, concat_axis=0, tiled=True)

    def shift(value, moves):
        return lax.ppermute(value, ("tile", "head"), moves)

    def exchange(to_down, to_up, with_relay):
        moves = direct if with_relay else steps
        down_pairs = pairs(moves)
        up_pairs = pairs([(u, t, h) for t, u, h in moves])
        if not with_relay:
            return shift(to_down, down_pairs), shift(to_up, up_pairs)
        relay = to_up if to_down is to_up else jnp.where(at_right, to_down, to_up)
        middle = shift(relay, first_pairs)
        from_up = shift(to_down, down_pairs)
        from_down = shift(to_up, up_pairs)
        return from_up, from_down, shift(middle, second_pairs)

    def edge_of(value):
        return lax.dynamic_slice_in_dim(value, edge_start, TILE_TOK, 0)

    def add_edge(value, term):
        return lax.dynamic_update_slice_in_dim(value, edge_of(value) + term, edge_start, 0)

    tokens = groups * queries.shape[0]
    packed = []
    for members in chunks:
        packed.append(pack(keys_in, values_in, cosine, sine, groups, members))
    every = tuple(range(sum(len(members) for members in chunks)))
    packed.append(pack(queries, grad_out, cosine, sine, groups, every))
    qg = across(packed[-1]).reshape(tokens, -1)
    query_side = []
    key_side = []
    for c, members in enumerate(chunks):
        kv = across(packed[c]).reshape(tokens, -1)
        with_relay = c in RELAYED
        up, down, *relay = exchange(kv, kv, with_relay)
        up_edge, down_edge = edge_of(up), edge_of(down)
        if with_relay:
            relay_edge = edge_of(relay[0])
            up_edge = jnp.where(relay_up, relay_edge, up_edge)
            down_edge = jnp.where(relay_down, relay_edge, down_edge)
        edges = jnp.concatenate([up_edge, edge_of(kv), down_edge], axis=0)
        edge = shift(edges, swap_pairs)
        out_q, own_g, up_g, down_g, edge_g = attend(
            place, members[0], qg, kv, up, down, edge, *relay
        )
        query_side.append(across(out_q.reshape(packed[c].shape)))
        back = shift(edge_g, swap_pairs)
        up_g = add_edge(up_g, back[:TILE_TOK])
        own_g = add_edge(own_g, back[TILE_TOK : 2 * TILE_TOK])
        down_g = add_edge(down_g, back[2 * TILE_TOK :])
        terms = (own_g,) + exchange(down_g, up_g, with_relay)
        total = sum(term.astype(F32) for term in terms).astype(BF16)
        key_side.append(across(total.reshape(packed[c].shape)))
    attended, query_grad = unpack(query_side, cosine, back_sine, groups, chunks, False)
    key_grad, value_grad = unpack(key_side, cosine, back_sine, groups, chunks, True)
    return attended, query_grad, key_grad, value_grad


def solution(mesh):
    tokens = P(("tile", "head"), None)
    return jax.shard_map(
        local,
        mesh=mesh,
        in_specs=(tokens, tokens, tokens, tokens, P(None, ("tile", "head"))),
        out_specs=(tokens, tokens, tokens, tokens),
        check_vma=False,
    )
```
